256 devices in a mesh: batch: 4 (over x), blk: 4 (over z_hi, core), uly: 16 (over y, z_lo).
Axes of the slice: x: 4, y: 4, z: 8 (z_hi: 2, z_lo: 4; z = z_hi * 4 + z_lo), core: 2. Of those that a mesh axis runs over, the one named last changes fastest.
Arguments:
- queries: bfloat16 [32768, 4096], P(('batch', 'blk', 'uly')), parts along dimension 0, may hold values from -6 to 6
- keys: bfloat16 [32768, 512], P(('batch', 'blk', 'uly')), parts along dimension 0, may hold values from -6 to 6
- values: bfloat16 [32768, 512], P(('batch', 'blk', 'uly')), parts along dimension 0, may hold values from -6 to 6
- saved_out: bfloat16 [32768, 4096], P(('batch', 'blk', 'uly')), parts along dimension 0, may hold values from -6 to 6
- out_grad: bfloat16 [32768, 4096], P(('batch', 'blk', 'uly')), parts along dimension 0, may hold values from -6 to 6
- doc_lengths: int32 [32], P('batch'), parts along dimension 0, may hold values from 1 to 4096, 8192 in all
Outputs:
- gradient_of_queries: bfloat16 [32768, 4096], P(('batch', 'blk', 'uly')), parts along dimension 0
- gradient_of_keys: bfloat16 [32768, 512], P(('batch', 'blk', 'uly')), parts along dimension 0
- gradient_of_values: bfloat16 [32768, 512], P(('batch', 'blk', 'uly')), parts along dimension 0
The draws below stay inside these ranges and needn't reach their ends.
There are 4 independent parts, one for each index of `batch`. The reference program is written for one: setup_inputs(seed, part) draws one part's arguments, and reference() takes and returns one part's arrays. A program takes and returns all parts, laid end to end along the dimension named above; each array names one. Nothing has to cross between parts.
Inputs may be any that keep to these rules, and one draw needn't show every extreme that they name: `doc_lengths`: the lengths sum to 8192 and the largest is exactly 4096.
All inputs are finite; a program needn't handle non-finite values.
Results may differ from the reference program's by a relative error of at most 0.0054.
Values may be sent and summed in bfloat16 or wider, within the bound.
No kernel may reach another device: no remote copies, remote signals or barrier semaphores. Data moves between devices by JAX's collectives and lax.ppermute only.
A program may use at most 64 MiB of HBM per device.

```python
import math
import jax
import jax.numpy as jnp
import numpy as np
from jax import lax

HEAD_SIZE = 128
QUERY_HEADS = 32
KEY_VALUE_HEADS = 4
DOCS = 8
WINDOW = 1024
SEQUENCE_TOKENS = 8192


def paired_fields(key):
    base = jax.random.fold_in(key, 11)
    key_q, key_projection = jax.random.split(base, 2)
    query_rows = jnp.clip(jax.random.normal(key_q, (SEQUENCE_TOKENS, QUERY_HEADS, HEAD_SIZE), jnp.float32), -6.0, 6.0)
    keyed_rows = jnp.clip(jax.random.normal(key_projection, (SEQUENCE_TOKENS, KEY_VALUE_HEADS, HEAD_SIZE), jnp.float32), -6.0, 6.0)
    return (query_rows.reshape(SEQUENCE_TOKENS, QUERY_HEADS * HEAD_SIZE), keyed_rows.reshape(SEQUENCE_TOKENS, KEY_VALUE_HEADS * HEAD_SIZE))


def draw_queries(key, part):
    return paired_fields(key)[0].astype(jnp.bfloat16)


def draw_keys(key, part):
    return paired_fields(key)[1].astype(jnp.bfloat16)


def level_of(key, dims, cuts, smallest, top_value):
    def one(axis_at, parts):
        steps = jax.random.uniform(jax.random.fold_in(jax.random.fold_in(key, 6), axis_at), (parts,), jnp.float32, smallest / len(cuts), top_value / len(cuts))
        return jnp.repeat(jnp.exp(steps), dims[axis_at] // parts).reshape((-1,) + (1,) * (len(dims) - axis_at - 1))

    level = one(*cuts[0])
    for cut in cuts[1:]:
        level = level * one(*cut)
    return level


def split_up(number_of, total, most, lean):
    weights = [(1 << 20) // math.isqrt(grade ** lean) + 1 for grade in range(2, number_of + 1)]
    rest, holding = total - most - (number_of - 1), [1] * (number_of - 1)
    while rest > 0:
        candidates = [i for i in range(number_of - 1) if holding[i] < most]
        mass, remaining = sum([weights[i] for i in candidates]), rest
        for i in candidates:
            extra = min(most - holding[i], max(1, remaining * weights[i] // mass), rest)
            holding[i] = holding[i] + extra
            rest = rest - extra
    return np.array([most] + holding)


def uneven_parts(rng, number_of, total, reach, skew):
    if number_of == 2:
        one = jax.random.randint(rng, (), max(1, total - reach), min(reach, total - 1) + 1)
        return jnp.stack([one, total - one])
    sizes = jnp.asarray(split_up(number_of, total, reach, skew), jnp.int32)
    couples = (number_of - 1) // 2
    source_of, receiver = sizes[1:1 + 2 * couples:2], sizes[2:2 + 2 * couples:2]
    margin = jnp.minimum(source_of - 1, reach - receiver)
    moved = jax.random.randint(jax.random.fold_in(rng, 1), (couples,), 0, 1 << 20) % (margin + 1)
    sizes = sizes.at[1:1 + 2 * couples:2].set(source_of - moved).at[2:2 + 2 * couples:2].set(receiver + moved)
    return sizes[jax.random.permutation(jax.random.fold_in(rng, 2), number_of)]


def normal_values(rng, shape, deviation, reach, shards=(), held_as=jnp.bfloat16):
    array = jax.random.normal(rng, shape, jnp.float32) * deviation
    if len(shards) > 0:
        array = level_of(rng, shape, shards, -0.22, 0.18) * array
    return jnp.clip(array, min=-reach, max=reach).astype(held_as)


def setup_inputs(seed: int = 0, part: int = 0) -> dict:
    streams_of = jax.random.split(jax.random.key(seed), 7)
    part_splits = jax.random.split(jax.random.fold_in(streams_of[6], part), 7)
    return {
        "queries": draw_queries(jax.random.fold_in(jax.random.fold_in(streams_of[6], part), 71), part),
        "keys": draw_keys(jax.random.fold_in(jax.random.fold_in(streams_of[6], part), 71), part),
        "values": normal_values(part_splits[2], (SEQUENCE_TOKENS, KEY_VALUE_HEADS * HEAD_SIZE), 1.0, 6.0, ((0, 64),)),
        "saved_out": normal_values(part_splits[3], (SEQUENCE_TOKENS, QUERY_HEADS * HEAD_SIZE), 1.0, 6.0, ((0, 64),)),
        "out_grad": normal_values(part_splits[4], (SEQUENCE_TOKENS, QUERY_HEADS * HEAD_SIZE), 1.0, 6.0, ((0, 64),)),
        "doc_lengths": uneven_parts(part_splits[5], DOCS, SEQUENCE_TOKENS, SEQUENCE_TOKENS // 2, 2).astype(jnp.int32),
    }


def reference(queries, keys, values, saved_out, out_grad, doc_lengths):
    group_width = QUERY_HEADS // KEY_VALUE_HEADS
    softmax_scale = HEAD_SIZE ** -0.5
    blocks = SEQUENCE_TOKENS // WINDOW
    bounds = jnp.cumsum(doc_lengths)[:-1]

    def document(positions):
        return jnp.sum((positions[..., None] >= bounds).astype(jnp.int32), axis=-1)

    block_ids = jnp.arange(blocks, dtype=jnp.int32)
    query_pos = block_ids[:, None] * WINDOW + jnp.arange(WINDOW, dtype=jnp.int32)[None, :]
    key_pos = (block_ids[:, None] - 1) * WINDOW + jnp.arange(2 * WINDOW, dtype=jnp.int32)[None, :]
    query_doc = document(query_pos)
    key_doc = document(jnp.maximum(key_pos, 0))
    qp = query_pos[:, :, None]
    kp = key_pos[:, None, :]
    allowed = (kp <= qp) & (kp > qp - WINDOW) & (kp >= 0) & (key_doc[:, None, :] == query_doc[:, :, None])

    products = jnp.sum(out_grad.astype(jnp.float32).reshape(SEQUENCE_TOKENS, QUERY_HEADS, HEAD_SIZE) * saved_out.astype(jnp.float32).reshape(SEQUENCE_TOKENS, QUERY_HEADS, HEAD_SIZE), axis=2)
    rounded = lax.optimization_barrier(products.astype(jnp.bfloat16))
    delta = rounded.astype(jnp.float32)

    def windows(block):
        padded = jnp.concatenate([jnp.zeros((WINDOW, HEAD_SIZE), block.dtype), block], axis=0).reshape(blocks + 1, WINDOW, HEAD_SIZE)
        return jnp.concatenate([padded[:-1], padded[1:]], axis=1)

    def fold_back(grads):
        tail = jnp.concatenate([grads[1:, :WINDOW], jnp.zeros((1, WINDOW, HEAD_SIZE), jnp.float32)], axis=0)
        return (grads[:, WINDOW:] + tail).reshape(SEQUENCE_TOKENS, HEAD_SIZE)

    def one_head(head):
        kv_head = (head // group_width).astype(jnp.int32)
        query_rows = lax.dynamic_slice_in_dim(queries, (head * HEAD_SIZE).astype(jnp.int32), HEAD_SIZE, 1)
        cotangent = lax.dynamic_slice_in_dim(out_grad, (head * HEAD_SIZE).astype(jnp.int32), HEAD_SIZE, 1)
        key_block = lax.dynamic_slice_in_dim(keys, (kv_head * HEAD_SIZE).astype(jnp.int32), HEAD_SIZE, 1)
        value_block = lax.dynamic_slice_in_dim(values, (kv_head * HEAD_SIZE).astype(jnp.int32), HEAD_SIZE, 1)
        delta_head = lax.dynamic_slice_in_dim(delta, head.astype(jnp.int32), 1, 1).reshape(blocks, WINDOW, 1)
        query_weight_matrix = query_rows.reshape(blocks, WINDOW, HEAD_SIZE).astype(jnp.float32)
        output_weight_gradient = cotangent.reshape(blocks, WINDOW, HEAD_SIZE).astype(jnp.float32)
        key_weight_matrix = windows(key_block).astype(jnp.float32)
        value_weight_matrix = windows(value_block).astype(jnp.float32)
        attention_logits = jnp.einsum("gjs,gns->gjn", query_weight_matrix, key_weight_matrix) * softmax_scale
        peak = jnp.max(jnp.where(allowed, attention_logits, -1e30), axis=2, keepdims=True)
        total = jnp.sum(jnp.where(allowed, jnp.exp(attention_logits - peak), 0.0), axis=2, keepdims=True)
        log_total = peak + jnp.log(total)
        probs = jnp.where(allowed, jnp.exp(attention_logits - log_total), 0.0)
        probability_lowered = probs.astype(jnp.bfloat16).astype(jnp.float32)
        gradient_of_values = jnp.einsum("lte,ltv->lev", probability_lowered, output_weight_gradient)
        probability_gradient = jnp.einsum("gjs,gns->gjn", output_weight_gradient, value_weight_matrix)
        score_gradient = (probs * (probability_gradient - delta_head)).astype(jnp.bfloat16).astype(jnp.float32)
        gradient_of_queries = jnp.einsum("rot,rtj->roj", score_gradient, key_weight_matrix) * softmax_scale
        gradient_of_keys = jnp.einsum("lte,ltv->lev", score_gradient, query_weight_matrix) * softmax_scale
        return gradient_of_queries.reshape(SEQUENCE_TOKENS, HEAD_SIZE), fold_back(gradient_of_keys), fold_back(gradient_of_values)

    head_ids = jnp.arange(QUERY_HEADS, dtype=jnp.int32)
    gradient_of_queries, gradient_of_keys, gradient_of_values = lax.map(one_head, head_ids)
    query_out = gradient_of_queries.transpose(1, 0, 2).reshape(SEQUENCE_TOKENS, QUERY_HEADS * HEAD_SIZE).astype(jnp.bfloat16)
    key_result = gradient_of_keys.reshape(KEY_VALUE_HEADS, group_width, SEQUENCE_TOKENS, HEAD_SIZE).sum(axis=1).transpose(1, 0, 2).reshape(SEQUENCE_TOKENS, KEY_VALUE_HEADS * HEAD_SIZE).astype(jnp.bfloat16)
    value_result = gradient_of_values.reshape(KEY_VALUE_HEADS, group_width, SEQUENCE_TOKENS, HEAD_SIZE).sum(axis=1).transpose(1, 0, 2).reshape(SEQUENCE_TOKENS, KEY_VALUE_HEADS * HEAD_SIZE).astype(jnp.bfloat16)
    return query_out, key_result, value_result
```

```python
import functools

import jax
import jax.numpy as jnp
import numpy as np
from jax import lax
from jax.experimental import pallas as pl
from jax.experimental.pallas import tpu as pltpu
from jax.sharding import Mesh
from jax.sharding import PartitionSpec as P

D = 128
T = 128
WINDOW = 1024
Y = 4
Z = 4
BACK = WINDOW // T
POS = BACK + Z * (Y - 1) + 1
ROWS = BACK // Z + Y
SPAN = (BACK + 1) * T
SCALE = D**-0.5
LOG2E = 1.4426950408889634
AXES = ("batch", "blk", "y", "z")


def pack_kv(k_ref, v_ref, o_ref):
    for h in range(Y):
        o_ref[h, :T] = k_ref[:, h * D : (h + 1) * D]
        o_ref[h, T:] = v_ref[:, h * D : (h + 1) * D]


def pack_rows(group, q_ref, s_ref, g_ref, qo_ref, go_ref):
    deltas = []
    for h in range(group):
        cols = slice(h * D, (h + 1) * D)
        qo_ref[0, h * T : (h + 1) * T] = q_ref[:, cols]
        grad = g_ref[:, cols]
        go_ref[0, h * T : (h + 1) * T] = grad
        product = grad.astype(jnp.float32) * s_ref[:, cols].astype(jnp.float32)
        deltas.append(jnp.sum(product.T, axis=0, keepdims=True))
    go_ref[0, group * T :] = jnp.concatenate(deltas, axis=0).astype(jnp.bfloat16)


def backward(
    group,
    doc_ref,
    q_ref,
    g_ref,
    x_ref,
    y1_ref,
    y2_ref,
    y3_ref,
    dq_ref,
    dx_ref,
    dy1_ref,
    dy2_ref,
    dy3_ref,
    k_scr,
    kt_scr,
    v_scr,
    dk_scr,
    dv_scr,
    s_scr,
    p_scr,
    ds_scr,
    delta_scr,
):
    k = pl.program_id(0)
    sources = (x_ref, y1_ref, y2_ref, y3_ref)

    @pl.when(k == 0)
    def _():
        for p in range(POS):
            m, d = divmod(p, Z)
            at = slice(p * T, (p + 1) * T)
            key = sources[d][m, :T]
            k_scr[at] = key
            kt_scr[:, at] = key.astype(jnp.float32).T.astype(jnp.bfloat16)
            v_scr[at] = sources[d][m, T:]
        dk_scr[...] = jnp.zeros_like(dk_scr)
        dv_scr[...] = jnp.zeros_like(dv_scr)

    delta_scr[...] = g_ref[0, group * T :, :].astype(jnp.float32)
    slab = Y * Z * T
    base = lax.axis_index("blk") * slab + (lax.axis_index("z") - BACK) * T
    first = pl.multiple_of(k * (Z * T), Z * T)
    query = first + WINDOW + lax.broadcasted_iota(jnp.int32, (1, T), 1)
    start = jnp.zeros((1, T), jnp.int32)
    bound = 0
    for c in range(7):
        bound = bound + doc_ref[c]
        start = jnp.where(query + base >= bound, bound, start)
    lowest = jnp.maximum(start - base, query - (WINDOW - 1)) - first
    lowest = jnp.concatenate([lowest, lowest], axis=1)
    key_at = lax.broadcasted_iota(jnp.int32, (T, 2 * T), 0)
    query_at = lax.broadcasted_iota(jnp.int32, (T, 2 * T), 1) & (T - 1)

    def pair(j, carry):
        at = pl.ds(pl.multiple_of(j * (2 * T), 2 * T), 2 * T)
        q2 = q_ref[0, at, :]
        g2 = g_ref[0, at, :]
        delta = jnp.concatenate(
            [
                delta_scr[pl.ds(2 * j, 1), :],
                delta_scr[pl.ds(2 * j + 1, 1), :],
            ],
            axis=1,
        )
        top = jnp.full((8, 2 * T), -1e30, jnp.float32)
        for c in range(BACK + 1):
            rows = slice(c * T, (c + 1) * T)
            keys = k_scr[pl.ds(pl.multiple_of(first + c * T, T), T), :]
            s = lax.dot_general(
                keys, q2, (((1,), (1,)), ((), ())), preferred_element_type=jnp.float32
            )
            allowed = key_at + c * T >= lowest
            if c == BACK:
                allowed = allowed & (key_at <= query_at)
            s = jnp.where(allowed, s, -1e30)
            s_scr[rows] = s
            for r in range(T // 8):
                top = jnp.maximum(top, s[r * 8 : (r + 1) * 8])
        peak = jnp.max(top, axis=0, keepdims=True) * (SCALE * LOG2E)
        total = jnp.zeros((8, 2 * T), jnp.float32)
        for c in range(BACK + 1):
            rows = slice(c * T, (c + 1) * T)
            e = jnp.exp2(s_scr[rows] * (SCALE * LOG2E) - peak)
            s_scr[rows] = e
            for r in range(T // 8):
                total = total + e[r * 8 : (r + 1) * 8]
        inverse = 1.0 / jnp.sum(total, axis=0, keepdims=True)
        for c in range(BACK + 1):
            rows = slice(c * T, (c + 1) * T)
            vals = v_scr[pl.ds(pl.multiple_of(first + c * T, T), T), :]
            dp = lax.dot_general(
                vals, g2, (((1,), (1,)), ((), ())), preferred_element_type=jnp.float32
            )
            p = s_scr[rows] * inverse
            p_scr[rows, at] = p.astype(jnp.bfloat16)
            ds_scr[rows, at] = (p * (dp - delta)).astype(jnp.bfloat16)
        return carry

    lax.fori_loop(0, group // 2, pair, 0)
    span = pl.ds(first, SPAN)
    dv_scr[span, :] += jnp.dot(
        p_scr[...], g_ref[0, : group * T, :], preferred_element_type=jnp.float32
    )
    dk_scr[span, :] += jnp.dot(
        ds_scr[...], q_ref[0], preferred_element_type=jnp.float32
    )
    dqt = jnp.dot(kt_scr[:, span], ds_scr[...], preferred_element_type=jnp.float32)
    for h in range(group):
        dq_ref[0, h * T : (h + 1) * T] = (
            (dqt[:, h * T : (h + 1) * T] * SCALE).T.astype(jnp.bfloat16)
        )

    @pl.when(k == Y - 1)
    def _():
        targets = (dx_ref, dy1_ref, dy2_ref, dy3_ref)
        for p in range(POS):
            m, d = divmod(p, Z)
            at = slice(p * T, (p + 1) * T)
            targets[d][m, :T] = (dk_scr[at] * SCALE).astype(targets[d].dtype)
            targets[d][m, T:] = dv_scr[at].astype(targets[d].dtype)


def combine(dx_ref, a_ref, b_ref, c_ref, own_ref, halo_ref, acc):
    z = lax.axis_index("z")
    acc[...] = dx_ref[...]
    for d, ref in ((1, a_ref), (2, b_ref), (3, c_ref)):
        off = (z < d).astype(jnp.int32)
        for m in range(ROWS - 1):
            acc[off + m] += ref[m].astype(jnp.float32)
    halo_ref[...] = acc[: BACK // Z].astype(jnp.bfloat16)
    own_ref[...] = acc[BACK // Z :]


def finish(own_ref, halo_ref, o_ref):
    for r in range(Y):
        total = own_ref[r]
        if r >= Y - BACK // Z:
            total = total + halo_ref[r - (Y - BACK // Z)].astype(jnp.float32)
        o_ref[r] = total.astype(jnp.bfloat16)


def vmem():
    return pl.BlockSpec(memory_space=pltpu.VMEM)


def on_device(queries, keys, values, saved_out, out_grad, doc_lengths):
    rows = queries.shape[0]
    group = queries.shape[1] // keys.shape[1]
    bf16, f32 = jnp.bfloat16, jnp.float32
    z = lax.axis_index("z")

    kv = pl.pallas_call(
        pack_kv,
        out_shape=jax.ShapeDtypeStruct((Y, 2 * T, D), bf16),
        in_specs=[vmem()] * 2,
        out_specs=vmem(),
    )(keys, values)
    own = lax.all_to_all(kv, "y", 0, 0, tiled=True)
    blks = lax.axis_size("blk")
    halo = lax.ppermute(
        own[Y - BACK // Z :], "blk", [(b, b + 1) for b in range(blks - 1)]
    )
    x = jnp.concatenate([halo, own], axis=0)

    wide = group * D
    q_out, g_out = pl.pallas_call(
        functools.partial(pack_rows, group),
        grid=(Y,),
        out_shape=(
            jax.ShapeDtypeStruct((Y, group * T, D), bf16),
            jax.ShapeDtypeStruct((Y, group * T + group, D), bf16),
        ),
        in_specs=[pl.BlockSpec((T, wide), lambda h: (0, h))] * 3,
        out_specs=(
            pl.BlockSpec((1, group * T, D), lambda h: (h, 0, 0)),
            pl.BlockSpec((1, group * T + group, D), lambda h: (h, 0, 0)),
        ),
    )(queries, saved_out, out_grad)
    q_all = lax.all_to_all(q_out, "y", 0, 0, tiled=True)
    g_all = lax.all_to_all(g_out, "y", 0, 0, tiled=True)

    def along(d):
        return [(i, (i - d) % Z) for i in range(Z)]

    def against(d):
        return [((i - d) % Z, i) for i in range(Z)]

    others = []
    for d in range(1, Z):
        part = lax.dynamic_slice_in_dim(x, (z < d).astype(jnp.int32), ROWS - 1, 0)
        others.append(lax.ppermute(part, "z", along(d)))

    def whole(shape):
        return pl.BlockSpec(shape, lambda k: (0,) * len(shape))

    part_shape = (ROWS - 1, 2 * T, D)
    x_shape = (ROWS, 2 * T, D)
    dq, dx, *dys = pl.pallas_call(
        functools.partial(backward, group),
        grid=(Y,),
        out_shape=(
            jax.ShapeDtypeStruct((Y, group * T, D), bf16),
            jax.ShapeDtypeStruct(x_shape, f32),
        )
        + (jax.ShapeDtypeStruct(part_shape, bf16),) * 3,
        in_specs=[
            pl.BlockSpec(memory_space=pltpu.SMEM),
            pl.BlockSpec((1, group * T, D), lambda k: (k, 0, 0)),
            pl.BlockSpec((1, group * T + group, D), lambda k: (k, 0, 0)),
            whole(x_shape),
        ]
        + [whole(part_shape)] * 3,
        out_specs=(pl.BlockSpec((1, group * T, D), lambda k: (k, 0, 0)), whole(x_shape))
        + (whole(part_shape),) * 3,
        scratch_shapes=[
            pltpu.VMEM((POS * T, D), bf16),
            pltpu.VMEM((D, POS * T), bf16),
            pltpu.VMEM((POS * T, D), bf16),
            pltpu.VMEM((POS * T, D), f32),
            pltpu.VMEM((POS * T, D), f32),
            pltpu.VMEM((SPAN, 2 * T), f32),
            pltpu.VMEM((SPAN, group * T), bf16),
            pltpu.VMEM((SPAN, group * T), bf16),
            pltpu.VMEM((group, T), f32),
        ],
        cost_estimate=pl.CostEstimate(
            flops=10 * Y * group * T * SPAN * D,
            transcendentals=Y * group * T * SPAN,
            bytes_accessed=8 << 20,
        ),
    )(doc_lengths, q_all, g_all, x, *others)

    dq_back = lax.all_to_all(dq, "y", 0, 0, tiled=True)
    dq_out = (
        dq_back.reshape(Y, group, T, D).transpose(2, 0, 1, 3).reshape(rows, Y * group * D)
    )

    backs = [lax.ppermute(dy, "z", against(d)) for d, dy in zip(range(1, Z), dys)]
    own_sum, halo_sum = pl.pallas_call(
        combine,
        out_shape=(
            jax.ShapeDtypeStruct((Y, 2 * T, D), f32),
            jax.ShapeDtypeStruct((BACK // Z, 2 * T, D), bf16),
        ),
        in_specs=[vmem()] * 4,
        out_specs=(vmem(), vmem()),
        scratch_shapes=[pltpu.VMEM(x_shape, f32)],
    )(dx, *backs)
    halo_back = lax.ppermute(halo_sum, "blk", [(b + 1, b) for b in range(blks - 1)])
    dkv = pl.pallas_call(
        finish,
        out_shape=jax.ShapeDtypeStruct((Y, 2 * T, D), bf16),
        in_specs=[vmem()] * 2,
        out_specs=vmem(),
    )(own_sum, halo_back)
    dkv = lax.all_to_all(dkv, "y", 0, 0, tiled=True)
    dkv = dkv.reshape(Y, 2, T, D).transpose(1, 2, 0, 3).reshape(2, rows, Y * D)
    return dq_out, dkv[0], dkv[1]


def solution(mesh):
    fine = Mesh(mesh.devices.reshape(4, 4, Y, Z), AXES)
    split = P(AXES, None)
    return jax.shard_map(
        on_device,
        mesh=fine,
        in_specs=(split,) * 5 + (P("batch"),),
        out_specs=(split,) * 3,
        check_vma=False,
    )
```

```python
import functools

import jax
import jax.numpy as jnp
import numpy as np
from jax import lax
from jax.experimental import pallas as pl
from jax.experimental.pallas import tpu as pltpu
from jax.sharding import Mesh
from jax.sharding import PartitionSpec as P

D = 128
T = 128
WINDOW = 1024
Y = 4
Z = 4
BACK = WINDOW // T
POS = BACK + Z * (Y - 1) + 1
ROWS = BACK // Z + Y
SPAN = (BACK + 1) * T
HALO = BACK // Z
EARLY = 3
PARTS = 2
SCALE = D**-0.5
LOG2E = 1.4426950408889634
AXES = ("batch", "blk", "y", "z")


def ring(e):
    return (lax.axis_index("y") + e) & (Y - 1)


def lanes(block, width):
    return pl.ds(pl.multiple_of(block * width, width), width)


def pack_kv(k_ref, v_ref, *outs):
    for e, out in enumerate(outs):
        cols = lanes(ring(e), D)
        out[:T] = k_ref[:, cols]
        out[T:] = v_ref[:, cols]


def arrange(a_ref, b_ref, c_ref, d_ref, own_ref, tail_ref, *lates):
    for e, ref in enumerate((a_ref, b_ref, c_ref, d_ref)):
        own_ref[pl.ds(ring(-e), 1)] = ref[...][None]
    tail_ref[...] = own_ref[Y - HALO :]
    z = lax.axis_index("z")
    for d, late in enumerate(lates, 1):
        count = late.shape[0]
        off = Y - count - 1 + (z < d).astype(jnp.int32)
        late[...] = own_ref[pl.ds(off, count)]


def arrange_early(own_ref, halo_ref, *earlies):
    z = lax.axis_index("z")
    for d, early in enumerate(earlies, 1):
        near = z < d

        @pl.when(near)
        def _():
            early[: HALO - 1] = halo_ref[1:]
            early[HALO - 1 :] = own_ref[: EARLY - HALO + 1]

        @pl.when(jnp.logical_not(near))
        def _():
            early[:HALO] = halo_ref[...]
            early[HALO:] = own_ref[: EARLY - HALO]


def pack_rows(heads, part, q_ref, s_ref, g_ref, *outs):
    for e, out in enumerate(outs):
        deltas = []
        for h in range(heads):
            cols = lanes((ring(e) * PARTS + part) * heads + h, D)
            out[h * T : (h + 1) * T] = q_ref[:, cols]
            grad = g_ref[:, cols]
            out[(heads + h) * T : (heads + h + 1) * T] = grad
            product = grad.astype(jnp.float32) * s_ref[:, cols].astype(jnp.float32)
            deltas.append(jnp.sum(product.T, axis=0, keepdims=True))
        deltas.append(jnp.zeros((8 - heads, T), jnp.float32))
        out[2 * heads * T :] = jnp.concatenate(deltas, axis=0).astype(jnp.bfloat16)


def key_block(p, own, halo, early, late):
    m, d = divmod(p, Z)
    if d == 0:
        return halo[m] if m < HALO else own[m - HALO]
    return early[d - 1][m] if m < EARLY else late[d - 1][m - EARLY]


def backward(heads, first_row, lo, hi, carried, final, left, *refs):
    refs = list(refs)
    doc_ref, *row_refs = refs[: 1 + Y]
    own, halo = refs[1 + Y : 3 + Y]
    early, late = refs[3 + Y : 6 + Y], refs[6 + Y : 9 + Y]
    refs = refs[9 + Y :]
    acc_in = []
    for _ in carried:
        acc_in.append((refs.pop(0), refs.pop(0)))
    dq_before, refs = (refs[:Y], refs[Y:]) if first_row else ([], refs)
    dq_refs, refs = refs[:Y], refs[Y:]
    targets = [refs.pop(0) for _ in range(Z)] if final else []
    acc_out = (refs.pop(0), refs.pop(0)) if left else ()
    k_scr, kt_scr, v_scr, dk_scr, dv_scr, s_scr, p_scr, ds_scr, delta_scr, row_ref, dq_ref = refs
    step = pl.program_id(0)

    @pl.when(step == 0)
    def _():
        for p in range(lo, hi):
            at = slice((p - lo) * T, (p - lo + 1) * T)
            block = key_block(p, own, halo, early, late)
            key = block[:T]
            k_scr[at] = key
            kt_scr[:, at] = key.astype(jnp.float32).T.astype(jnp.bfloat16)
            v_scr[at] = block[T:]
        for before, dq_out in zip(dq_before, dq_refs):
            dq_out[...] = before[...]
        if not carried:
            dk_scr[...] = jnp.zeros_like(dk_scr)
            dv_scr[...] = jnp.zeros_like(dv_scr)
        for (begin, end, base), (dk_in, dv_in) in zip(carried, acc_in):
            to = slice((begin - lo) * T, (end - lo) * T)
            at = slice((begin - base) * T, (end - base) * T)
            dk_scr[to] = dk_in[at]
            dv_scr[to] = dv_in[at]

    source = ring(-first_row - step)
    for e in range(Y):

        @pl.when(source == e)
        def _():
            row_ref[...] = row_refs[e][...]

    delta_scr[...] = row_ref[2 * heads * T :, :].astype(jnp.float32)
    slab = Y * Z * T
    base = lax.axis_index("blk") * slab + (lax.axis_index("z") - BACK + lo) * T
    first = pl.multiple_of(step * (Z * T), Z * T)
    query = first + WINDOW + lax.broadcasted_iota(jnp.int32, (1, T), 1)
    start = jnp.zeros((1, T), jnp.int32)
    bound = 0
    for c in range(7):
        bound = bound + doc_ref[c]
        start = jnp.where(query + base >= bound, bound, start)
    lowest = jnp.maximum(start - base, query - (WINDOW - 1)) - first
    lowest = jnp.concatenate([lowest, lowest], axis=1)
    key_at = lax.broadcasted_iota(jnp.int32, (T, 2 * T), 0)
    query_at = lax.broadcasted_iota(jnp.int32, (T, 2 * T), 1) & (T - 1)

    def pair(j, carry):
        at = pl.ds(pl.multiple_of(j * (2 * T), 2 * T), 2 * T)
        q2 = row_ref[at, :]
        g2 = row_ref[pl.ds(pl.multiple_of(heads * T + j * (2 * T), 2 * T), 2 * T), :]
        delta = jnp.concatenate(
            [delta_scr[pl.ds(2 * j, 1), :], delta_scr[pl.ds(2 * j + 1, 1), :]], axis=1
        )
        top = jnp.full((8, 2 * T), -1e30, jnp.float32)
        for c in range(BACK + 1):
            rows = slice(c * T, (c + 1) * T)
            keys = k_scr[pl.ds(pl.multiple_of(first + c * T, T), T), :]
            s = lax.dot_general(
                keys, q2, (((1,), (1,)), ((), ())), preferred_element_type=jnp.float32
            )
            allowed = key_at + c * T >= lowest
            if c == BACK:
                allowed = allowed & (key_at <= query_at)
            s = jnp.where(allowed, s, -1e30)
            s_scr[rows] = s
            for r in range(T // 8):
                top = jnp.maximum(top, s[r * 8 : (r + 1) * 8])
        peak = jnp.max(top, axis=0, keepdims=True) * (SCALE * LOG2E)
        total = jnp.zeros((8, 2 * T), jnp.float32)
        for c in range(BACK + 1):
            rows = slice(c * T, (c + 1) * T)
            e = jnp.exp2(s_scr[rows] * (SCALE * LOG2E) - peak)
            s_scr[rows] = e
            for r in range(T // 8):
                total = total + e[r * 8 : (r + 1) * 8]
        inverse = 1.0 / jnp.sum(total, axis=0, keepdims=True)
        for c in range(BACK + 1):
            rows = slice(c * T, (c + 1) * T)
            vals = v_scr[pl.ds(pl.multiple_of(first + c * T, T), T), :]
            dp = lax.dot_general(
                vals, g2, (((1,), (1,)), ((), ())), preferred_element_type=jnp.float32
            )
            p = s_scr[rows] * inverse
            p_scr[rows, at] = p.astype(jnp.bfloat16)
            ds_scr[rows, at] = (p * (dp - delta)).astype(jnp.bfloat16)
        return carry

    lax.fori_loop(0, heads // 2, pair, 0)
    span = pl.ds(first, SPAN)
    dv_scr[span, :] += jnp.dot(
        p_scr[...],
        row_ref[heads * T : 2 * heads * T, :],
        preferred_element_type=jnp.float32,
    )
    dk_scr[span, :] += jnp.dot(
        ds_scr[...], row_ref[: heads * T, :], preferred_element_type=jnp.float32
    )
    dqt = jnp.dot(kt_scr[:, span], ds_scr[...], preferred_element_type=jnp.float32)
    for h in range(heads):
        dq_ref[h * T : (h + 1) * T] = (
            (dqt[:, h * T : (h + 1) * T] * SCALE).T.astype(jnp.bfloat16)
        )

    for e in range(Y):

        @pl.when(source == e)
        def _():
            dq_refs[e][...] = dq_ref[...]

    @pl.when(step == pl.num_programs(0) - 1)
    def _():
        for p in range(*final) if final else ():
            m, d = divmod(p - final[0], Z)
            at = slice((p - lo) * T, (p - lo + 1) * T)
            target = targets[d]
            target[m, :T] = (dk_scr[at] * SCALE).astype(target.dtype)
            target[m, T:] = dv_scr[at].astype(target.dtype)
        if left:
            at = slice((left[0] - lo) * T, (left[1] - lo) * T)
            acc_out[0][...] = dk_scr[at]
            acc_out[1][...] = dv_scr[at]


def halo_sum(dx_ref, a_ref, b_ref, c_ref, o_ref, acc):
    z = lax.axis_index("z")
    acc[:HALO] = dx_ref[...]
    for d, ref in ((1, a_ref), (2, b_ref), (3, c_ref)):
        off = (z < d).astype(jnp.int32)
        for m in range(HALO):
            acc[off + m] += ref[m].astype(jnp.float32)
    o_ref[...] = acc[:HALO].astype(jnp.bfloat16)


def own_sum(dx_ref, a_ref, b_ref, c_ref, d_ref, e_ref, f_ref, halo_ref, *rest):
    *outs, acc = rest
    z = lax.axis_index("z")
    acc[:HALO] = jnp.zeros((HALO, 2 * T, D), jnp.float32)
    acc[HALO:] = dx_ref[...]
    for d, (ref, more) in ((1, (a_ref, d_ref)), (2, (b_ref, e_ref)), (3, (c_ref, f_ref))):
        off = (z < d).astype(jnp.int32)
        acc[off + HALO - 1] += ref[HALO - 1].astype(jnp.float32)
        for m in range(ROWS - 1 - HALO):
            acc[off + HALO + m] += more[m].astype(jnp.float32)
    acc[ROWS - HALO :] += halo_ref[...].astype(jnp.float32)
    for e, out in enumerate(outs):
        out[...] = acc[HALO + ring(-e)].astype(jnp.bfloat16)


def unpack_q(heads, *refs):
    *parts, o_ref = refs
    for i, ref in enumerate(parts):
        part, e = divmod(i, Y)
        for h in range(heads):
            cols = lanes((ring(e) * PARTS + part) * heads + h, D)
            o_ref[:, cols] = ref[h * T : (h + 1) * T]


def unpack_kv(a_ref, b_ref, c_ref, d_ref, k_ref, v_ref):
    for e, ref in enumerate((a_ref, b_ref, c_ref, d_ref)):
        cols = lanes(ring(e), D)
        k_ref[:, cols] = ref[:T]
        v_ref[:, cols] = ref[T:]


def vmem():
    return pl.BlockSpec(memory_space=pltpu.VMEM)


def whole(shape):
    return pl.BlockSpec(shape, lambda *_: (0,) * len(shape))


def limit(mib):
    return pltpu.CompilerParams(vmem_limit_bytes=mib << 20)


def on_device(queries, keys, values, saved_out, out_grad, doc_lengths):
    rows = queries.shape[0]
    group = queries.shape[1] // keys.shape[1]
    heads = group // PARTS
    bf16, f32 = jnp.bfloat16, jnp.float32
    z = lax.axis_index("z")
    blks = lax.axis_size("blk")
    block = (2 * T, D)

    def along(d):
        return [(i, (i - d) % Z) for i in range(Z)]

    def against(d):
        return [((i - d) % Z, i) for i in range(Z)]

    def out_of(e):
        return [(i, (i + e) % Y) for i in range(Y)]

    def back_from(e):
        return [((i + e) % Y, i) for i in range(Y)]

    def shape(*dims, dtype=bf16):
        return jax.ShapeDtypeStruct(dims, dtype)

    def simple(body, shapes, count, mib, scratch=()):
        return pl.pallas_call(
            body,
            out_shape=shapes,
            in_specs=[vmem()] * count,
            out_specs=jax.tree.map(lambda _: vmem(), shapes),
            scratch_shapes=scratch,
            compiler_params=limit(mib),
        )

    def swap(pieces, pairs, name):
        with jax.named_scope(name):
            return [pieces[0]] + [
                lax.ppermute(pieces[e], "y", pairs(e)) for e in range(1, Y)
            ]

    count = ROWS - 1 - EARLY
    kv = simple(pack_kv, [shape(*block)] * Y, 2, 4)(keys, values)
    kv = swap(kv, out_of, "kvin")
    own, tail, *lates = simple(
        arrange,
        [shape(Y, *block), shape(HALO, *block)] + [shape(count, *block)] * (Z - 1),
        Y,
        4,
    )(*kv)
    with jax.named_scope("haloin"):
        halo = lax.ppermute(tail, "blk", [(b, b + 1) for b in range(blks - 1)])
    late = []
    for d in range(1, Z):
        with jax.named_scope(f"late{d}"):
            late.append(lax.ppermute(lates[d - 1], "z", along(d)))
    earlies = simple(arrange_early, [shape(EARLY, *block)] * (Z - 1), 2, 4)(own, halo)
    early = []
    for d in range(1, Z):
        with jax.named_scope(f"early{d}"):
            early.append(lax.ppermute(earlies[d - 1], "z", along(d)))

    tall = 2 * heads * T + 8
    moved = []
    for part in range(PARTS):
        packed = simple(
            functools.partial(pack_rows, heads, part), [shape(tall, D)] * Y, 3, 12
        )(queries, saved_out, out_grad)
        moved.append(swap(packed, out_of, f"qin{part}"))

    def run(row, first_row, count, lo, hi, carried, accs, final, left, dq):
        operands = [doc_lengths, *row, own, halo, *early, *late]
        in_specs = [pl.BlockSpec(memory_space=pltpu.SMEM)]
        in_specs += [vmem() for a in operands[1:]]
        for a in accs:
            operands.append(a)
            in_specs.append(vmem())
        if first_row:
            for e in range(Y):
                operands.append(dq[e])
                in_specs.append(vmem())
        shapes = [jax.ShapeDtypeStruct((heads * T, D), bf16)] * Y
        out_specs = [vmem()] * Y
        if final:
            span = final[1] - final[0]
            for d in range(Z):
                shape = ((span - d + Z - 1) // Z, *block)
                shapes.append(jax.ShapeDtypeStruct(shape, bf16 if d else f32))
                out_specs.append(vmem())
        if left:
            for _ in range(2):
                shape = ((left[1] - left[0]) * T, D)
                shapes.append(jax.ShapeDtypeStruct(shape, f32))
                out_specs.append(vmem())
        held = (hi - lo) * T
        return pl.pallas_call(
            functools.partial(
                backward, heads, first_row, lo, hi, carried, final, left
            ),
            grid=(count,),
            out_shape=shapes,
            in_specs=in_specs,
            out_specs=out_specs,
            scratch_shapes=[
                pltpu.VMEM((held, D), bf16),
                pltpu.VMEM((D, held), bf16),
                pltpu.VMEM((held, D), bf16),
                pltpu.VMEM((held, D), f32),
                pltpu.VMEM((held, D), f32),
                pltpu.VMEM((SPAN, 2 * T), f32),
                pltpu.VMEM((SPAN, heads * T), bf16),
                pltpu.VMEM((SPAN, heads * T), bf16),
                pltpu.VMEM((8, T), f32),
                pltpu.VMEM((tall, D), bf16),
                pltpu.VMEM((heads * T, D), bf16),
            ],
            compiler_params=limit(20),
            cost_estimate=pl.CostEstimate(
                flops=10 * count * heads * T * SPAN * D,
                transcendentals=count * heads * T * SPAN,
                bytes_accessed=8 << 20,
            ),
        )(*operands)

    cut = HALO * Z
    shared = BACK + Z + 1
    *dq_a, dk, dv = run(moved[0], 0, Y, 0, POS, (), (), None, (0, POS), None)
    *dq_b, dx1, dy1_1, dy1_2, dy1_3, dk1, dv1 = run(
        moved[1],
        0,
        2,
        0,
        shared,
        ((0, shared, 0),),
        (dk, dv),
        (0, cut),
        (cut, shared),
        None,
    )
    *dq_b, dx2, dy2_1, dy2_2, dy2_3 = run(
        moved[1],
        2,
        2,
        cut,
        POS,
        ((cut, shared, cut), (shared, POS, 0)),
        (dk1, dv1, dk, dv),
        (cut, POS),
        None,
        dq_b,
    )

    back1, back2 = [], []
    for d in range(1, Z):
        with jax.named_scope(f"outa{d}"):
            back1.append(lax.ppermute((dy1_1, dy1_2, dy1_3)[d - 1], "z", against(d)))
    for d in range(1, Z):
        with jax.named_scope(f"outb{d}"):
            back2.append(lax.ppermute((dy2_1, dy2_2, dy2_3)[d - 1], "z", against(d)))
    halo_out = pl.pallas_call(
        halo_sum,
        out_shape=jax.ShapeDtypeStruct((HALO, *block), bf16),
        in_specs=[vmem()] * 4,
        out_specs=vmem(),
        scratch_shapes=[pltpu.VMEM((HALO + 1, *block), f32)],
        compiler_params=limit(4),
    )(dx1, *back1)
    with jax.named_scope("haloout"):
        halo_back = lax.ppermute(halo_out, "blk", [(b + 1, b) for b in range(blks - 1)])
    back_a = swap(dq_a, back_from, "qout0")
    back_b = swap(dq_b, back_from, "qout1")
    dkv = simple(
        own_sum, [shape(*block)] * Y, 8, 8, [pltpu.VMEM((ROWS, *block), f32)]
    )(dx2, *back1, *back2, halo_back)
    dkv = swap(dkv, back_from, "kvout")
    dq_out = simple(
        functools.partial(unpack_q, heads), shape(rows, Y * group * D), PARTS * Y, 8
    )(*back_a, *back_b)
    dk_out, dv_out = simple(unpack_kv, [shape(rows, Y * D)] * 2, Y, 4)(*dkv)
    return dq_out, dk_out, dv_out


def solution(mesh):
    fine = Mesh(mesh.devices.reshape(4, 4, Y, Z), AXES)
    split = P(AXES, None)
    return jax.shard_map(
        on_device,
        mesh=fine,
        in_specs=(split,) * 5 + (P("batch"),),
        out_specs=(split,) * 3,
        check_vma=False,
    )
```

```python
import functools

import jax
import jax.numpy as jnp
from jax import lax
from jax.experimental import pallas as pl
from jax.experimental.pallas import tpu as pltpu
from jax.sharding import Mesh
from jax.sharding import PartitionSpec as P


D = 128
T = 128
WINDOW = 1024
Y = 4
Z = 4
BACK = WINDOW // T
POS = BACK + Z * (Y - 1) + 1
ROWS = BACK // Z + Y
SPAN = (BACK + 1) * T
HALO = BACK // Z
EARLY = 2
PARTS = 2
SCALE = D**-0.5
LOG2E = 1.4426950408889634
AXES = ("batch", "blk", "y", "z")


def ring(e):
    return (lax.axis_index("y") + e) & (Y - 1)


def lanes(block, width):
    return pl.ds(pl.multiple_of(block * width, width), width)


def pack_kv(k_hbm, v_hbm, *refs):
    *outs, k_buf, v_buf, sems = refs
    copies = [
        pltpu.make_async_copy(k_hbm, k_buf, sems.at[0]),
        pltpu.make_async_copy(v_hbm, v_buf, sems.at[1]),
    ]
    for copy in copies:
        copy.start()
    for copy in copies:
        copy.wait()
    for e, out in enumerate(outs):
        cols = lanes(ring(e), D)
        out[:T] = k_buf[:, cols]
        out[T:] = v_buf[:, cols]


def arrange(a_ref, b_ref, c_ref, d_ref, own_ref, tail_ref, *lates):
    for e, ref in enumerate((a_ref, b_ref, c_ref, d_ref)):
        own_ref[pl.ds(ring(-e), 1)] = ref[...][None]
    tail_ref[...] = own_ref[Y - HALO :]
    z = lax.axis_index("z")
    for d, late in enumerate(lates, 1):
        count = late.shape[0]
        off = Y - count - 1 + (z < d).astype(jnp.int32)
        late[...] = own_ref[pl.ds(off, count)]


def arrange_early(own_ref, halo_ref, *earlies):
    z = lax.axis_index("z")
    for d, early in enumerate(earlies, 1):
        near = z < d

        @pl.when(near)
        def _():
            early[: HALO - 1] = halo_ref[1:]
            early[HALO - 1 :] = own_ref[: EARLY - HALO + 1]

        @pl.when(jnp.logical_not(near))
        def _():
            early[...] = halo_ref[...]


def pack_rows(heads, part, q_hbm, s_hbm, g_hbm, *refs):
    *outs, q_buf, s_buf, g_buf, sems = refs
    wide = heads * D
    copies = []
    for e in range(len(outs)):
        cols = lanes(ring(e) * PARTS + part, wide)
        for i, (hbm, buf) in enumerate(
            ((g_hbm, g_buf), (s_hbm, s_buf), (q_hbm, q_buf))
        ):
            copies.append(
                pltpu.make_async_copy(hbm.at[:, cols], buf.at[e], sems.at[e, i])
            )
            copies[-1].start()
    for e, out in enumerate(outs):
        for copy in copies[3 * e : 3 * e + 3]:
            copy.wait()
        deltas = []
        for h in range(heads):
            cols = slice(h * D, (h + 1) * D)
            out[h * T : (h + 1) * T] = q_buf[e, :, cols]
            grad = g_buf[e, :, cols]
            out[(heads + h) * T : (heads + h + 1) * T] = grad
            product = grad.astype(jnp.float32) * s_buf[e, :, cols].astype(jnp.float32)
            deltas.append(jnp.sum(product.T, axis=0, keepdims=True))
        deltas.append(jnp.zeros((8 - heads, T), jnp.float32))
        out[2 * heads * T :] = jnp.concatenate(deltas, axis=0).astype(jnp.bfloat16)


def key_block(p, own, halo, early, late):
    m, d = divmod(p, Z)
    if d == 0:
        return halo[m] if m < HALO else own[m - HALO]
    return early[d - 1][m] if m < EARLY else late[d - 1][m - EARLY]


def backward(heads, first_row, lo, hi, carried, final, left, *refs):
    refs = list(refs)
    doc_ref, *row_refs = refs[: 1 + Y]
    own, halo = refs[1 + Y : 3 + Y]
    early, late = refs[3 + Y : 6 + Y], refs[6 + Y : 9 + Y]
    refs = refs[9 + Y :]
    acc_in = []
    for _ in carried:
        acc_in.append((refs.pop(0), refs.pop(0)))
    dq_before, refs = (refs[:Y], refs[Y:]) if first_row else ([], refs)
    dq_refs, refs = refs[:Y], refs[Y:]
    targets = [refs.pop(0) for _ in range(Z)] if final else []
    acc_out = (refs.pop(0), refs.pop(0)) if left else ()
    k_scr, kt_scr, v_scr, dk_scr, dv_scr, s_scr, p_scr, ds_scr, delta_scr, row_ref, dq_ref = refs
    step = pl.program_id(0)

    @pl.when(step == 0)
    def _():
        for p in range(lo, hi):
            at = slice((p - lo) * T, (p - lo + 1) * T)
            block = key_block(p, own, halo, early, late)
            key = block[:T]
            k_scr[at] = key
            kt_scr[:, at] = key.astype(jnp.float32).T.astype(jnp.bfloat16)
            v_scr[at] = block[T:]
        for before, dq_out in zip(dq_before, dq_refs):
            dq_out[...] = before[...]
        if not carried:
            dk_scr[...] = jnp.zeros_like(dk_scr)
            dv_scr[...] = jnp.zeros_like(dv_scr)
        for (begin, end, base), (dk_in, dv_in) in zip(carried, acc_in):
            to = slice((begin - lo) * T, (end - lo) * T)
            at = slice((begin - base) * T, (end - base) * T)
            dk_scr[to] = dk_in[at]
            dv_scr[to] = dv_in[at]

    source = ring(-first_row - step)
    for e in range(Y):

        @pl.when(source == e)
        def _():
            row_ref[...] = row_refs[e][...]

    delta_scr[...] = row_ref[2 * heads * T :, :].astype(jnp.float32)
    slab = Y * Z * T
    base = lax.axis_index("blk") * slab + (lax.axis_index("z") - BACK + lo) * T
    first = pl.multiple_of(step * (Z * T), Z * T)
    query = first + WINDOW + lax.broadcasted_iota(jnp.int32, (1, T), 1)
    start = jnp.zeros((1, T), jnp.int32)
    bound = 0
    for c in range(7):
        bound = bound + doc_ref[c]
        start = jnp.where(query + base >= bound, bound, start)
    lowest = jnp.maximum(start - base, query - (WINDOW - 1)) - first
    lowest = jnp.concatenate([lowest, lowest], axis=1)
    key_at = lax.broadcasted_iota(jnp.int32, (T, 2 * T), 0)
    query_at = lax.broadcasted_iota(jnp.int32, (T, 2 * T), 1) & (T - 1)

    span = pl.ds(first, SPAN)

    def scores(j):
        at = slice(j * 2 * T, (j + 1) * 2 * T)
        s_all = lax.dot_general(
            k_scr[span, :],
            row_ref[at, :],
            (((1,), (1,)), ((), ())),
            preferred_element_type=jnp.float32,
        )
        top = jnp.full((8, 2 * T), -1e30, jnp.float32)
        for c in range(BACK + 1):
            rows = slice(c * T, (c + 1) * T)
            allowed = key_at >= lowest - c * T
            if c == BACK:
                allowed = allowed & (key_at <= query_at)
            s = jnp.where(allowed, s_all[rows], -1e30)
            s_scr[j % 2, rows] = s
            for r in range(T // 8):
                top = jnp.maximum(top, s[r * 8 : (r + 1) * 8])
        return jnp.max(top, axis=0, keepdims=True) * (SCALE * LOG2E)

    def exponentials(j, peak):
        total = jnp.zeros((8, 2 * T), jnp.float32)
        for c in range(BACK + 1):
            rows = slice(c * T, (c + 1) * T)
            e = jnp.exp2(s_scr[j % 2, rows] * (SCALE * LOG2E) - peak)
            s_scr[j % 2, rows] = e
            for r in range(T // 8):
                total = total + e[r * 8 : (r + 1) * 8]
        return 1.0 / jnp.sum(total, axis=0, keepdims=True)

    def gradients(j, inverse):
        delta = jnp.concatenate(
            [delta_scr[2 * j : 2 * j + 1], delta_scr[2 * j + 1 : 2 * j + 2]], axis=1
        )
        dp_all = lax.dot_general(
            v_scr[span, :],
            row_ref[heads * T + j * 2 * T : heads * T + (j + 1) * 2 * T, :],
            (((1,), (1,)), ((), ())),
            preferred_element_type=jnp.float32,
        )
        for c in range(BACK + 1):
            rows = slice(c * T, (c + 1) * T)
            p = s_scr[j % 2, rows] * inverse
            ds = p * (dp_all[rows] - delta)
            for i in range(2):
                cols = slice(i * T, (i + 1) * T)
                p_scr[2 * j + i, rows] = p[:, cols].astype(jnp.bfloat16)
                ds_scr[2 * j + i, rows] = ds[:, cols].astype(jnp.bfloat16)

    def joined(ref, heads_of):
        return jnp.concatenate([ref[h] for h in heads_of], axis=1)

    def products(heads_of):
        n = len(heads_of)
        at = heads_of[0] * T
        dv_scr[span, :] += jnp.dot(
            joined(p_scr, heads_of),
            row_ref[heads * T + at : heads * T + at + n * T, :],
            preferred_element_type=jnp.float32,
        )
        ds = joined(ds_scr, heads_of)
        dk_scr[span, :] += jnp.dot(
            ds, row_ref[at : at + n * T, :], preferred_element_type=jnp.float32
        )
        dqt = jnp.dot(kt_scr[:, span], ds, preferred_element_type=jnp.float32)
        for i, h in enumerate(heads_of):
            dq_ref[h * T : (h + 1) * T] = (
                (dqt[:, i * T : (i + 1) * T] * SCALE).T.astype(jnp.bfloat16)
            )

    pairs = heads // 2
    inverse = exponentials(0, scores(0))
    for j in range(pairs):
        peak = scores(j + 1) if j + 1 < pairs else None
        gradients(j, inverse)
        if j + 1 < pairs:
            inverse = exponentials(j + 1, peak)
    products(range(heads))

    for e in range(Y):

        @pl.when(source == e)
        def _():
            dq_refs[e][...] = dq_ref[...]

    @pl.when(step == pl.num_programs(0) - 1)
    def _():
        for p in range(*final) if final else ():
            m, d = divmod(p - final[0], Z)
            at = slice((p - lo) * T, (p - lo + 1) * T)
            target = targets[d]
            target[m, :T] = (dk_scr[at] * SCALE).astype(target.dtype)
            target[m, T:] = dv_scr[at].astype(target.dtype)
        if left:
            at = slice((left[0] - lo) * T, (left[1] - lo) * T)
            acc_out[0][...] = dk_scr[at]
            acc_out[1][...] = dv_scr[at]


def halo_sum(dx_ref, a_ref, b_ref, c_ref, o_ref, acc):
    z = lax.axis_index("z")
    acc[:HALO] = dx_ref[...]
    for d, ref in ((1, a_ref), (2, b_ref), (3, c_ref)):
        off = (z < d).astype(jnp.int32)
        for m in range(HALO):
            acc[off + m] += ref[m].astype(jnp.float32)
    o_ref[...] = acc[:HALO].astype(jnp.bfloat16)


def own_sum(dx_ref, more_ref, halo_ref, far_ref, *refs):
    backs, outs, acc = refs[: 3 * (Z - 1)], refs[3 * (Z - 1) : -1], refs[-1]
    z = lax.axis_index("z")
    acc[:HALO] = jnp.zeros((HALO, 2 * T, D), jnp.float32)
    acc[HALO : HALO + 1] = dx_ref[...]
    acc[HALO + 1 :] = more_ref[...]
    for d in range(1, Z):
        off = (z < d).astype(jnp.int32)
        one, two, three = backs[d - 1 :: Z - 1]
        acc[off + HALO - 1] += one[HALO - 1].astype(jnp.float32)
        acc[off + HALO] += two[0].astype(jnp.float32)
        for m in range(three.shape[0]):
            acc[off + HALO + 1 + m] += three[m].astype(jnp.float32)
    acc[ROWS - HALO :] += (halo_ref[...] + far_ref[...]).astype(jnp.float32)
    for e, out in enumerate(outs):
        out[...] = acc[HALO + ring(-e)].astype(jnp.bfloat16)


def unpack_q(heads, *refs):
    *parts, o_ref = refs
    for i, ref in enumerate(parts):
        part, e = divmod(i, Y)
        for h in range(heads):
            cols = lanes((ring(e) * PARTS + part) * heads + h, D)
            o_ref[:, cols] = ref[h * T : (h + 1) * T]


def unpack_kv(a_ref, b_ref, c_ref, d_ref, k_ref, v_ref):
    for e, ref in enumerate((a_ref, b_ref, c_ref, d_ref)):
        cols = lanes(ring(e), D)
        k_ref[:, cols] = ref[:T]
        v_ref[:, cols] = ref[T:]


def vmem():
    return pl.BlockSpec(memory_space=pltpu.VMEM)


def limit(mib):
    return pltpu.CompilerParams(vmem_limit_bytes=mib << 20)


def on_device(queries, keys, values, saved_out, out_grad, doc_lengths):
    rows = queries.shape[0]
    group = queries.shape[1] // keys.shape[1]
    heads = group // PARTS
    bf16, f32 = jnp.bfloat16, jnp.float32
    blks = lax.axis_size("blk")
    block = (2 * T, D)

    def along(d):
        return [(i, (i - d) % Z) for i in range(Z)]

    def against(d):
        return [((i - d) % Z, i) for i in range(Z)]

    def out_of(e):
        return [(i, (i + e) % Y) for i in range(Y)]

    def back_from(e):
        return [((i + e) % Y, i) for i in range(Y)]

    def shape(*dims, dtype=bf16):
        return jax.ShapeDtypeStruct(dims, dtype)

    def simple(body, shapes, count, mib, scratch=()):
        return pl.pallas_call(
            body,
            out_shape=shapes,
            in_specs=[vmem()] * count,
            out_specs=jax.tree.map(lambda _: vmem(), shapes),
            scratch_shapes=scratch,
            compiler_params=limit(mib),
        )

    def swap(pieces, pairs):
        out = [pieces[0]]
        for e in range(1, Y):
            out.append(lax.ppermute(pieces[e], "y", pairs(e)))
        return out

    count = ROWS - 1 - EARLY
    kv = pl.pallas_call(
        pack_kv,
        out_shape=[shape(*block)] * Y,
        in_specs=[pl.BlockSpec(memory_space=pltpu.HBM)] * 2,
        out_specs=[vmem()] * Y,
        scratch_shapes=[pltpu.VMEM((T, Y * D), bf16)] * 2
        + [pltpu.SemaphoreType.DMA((2,))],
        compiler_params=limit(56),
    )(keys, values)
    kv = swap(kv, out_of)
    own, tail, *lates = simple(
        arrange,
        [shape(Y, *block), shape(HALO, *block)] + [shape(count, *block)] * (Z - 1),
        Y,
        4,
    )(*kv)
    halo = lax.ppermute(tail, "blk", [(b, b + 1) for b in range(blks - 1)])
    late = []
    for d in range(1, Z):
        late.append(lax.ppermute(lates[d - 1], "z", along(d)))
    earlies = simple(arrange_early, [shape(EARLY, *block)] * (Z - 1), 2, 4)(own, halo)
    early = []
    for d in range(1, Z):
        early.append(lax.ppermute(earlies[d - 1], "z", along(d)))

    tall = 2 * heads * T + 8
    moved = []
    for part in range(PARTS):
        packed = pl.pallas_call(
            functools.partial(pack_rows, heads, part),
            out_shape=[shape(tall, D)] * Y,
            in_specs=[pl.BlockSpec(memory_space=pltpu.HBM)] * 3,
            out_specs=[vmem()] * Y,
            scratch_shapes=[pltpu.VMEM((Y, T, heads * D), bf16)] * 3
            + [pltpu.SemaphoreType.DMA((Y, 3))],
            compiler_params=limit(56),
        )(queries, saved_out, out_grad)
        moved.append(swap(packed, out_of))

    def run(row, first_row, count, lo, hi, carried, accs, final, left, dq):
        operands = [doc_lengths, *row, own, halo, *early, *late]
        in_specs = [pl.BlockSpec(memory_space=pltpu.SMEM)]
        in_specs += [vmem() for a in operands[1:]]
        for a in accs:
            operands.append(a)
            in_specs.append(vmem())
        if first_row:
            for e in range(Y):
                operands.append(dq[e])
                in_specs.append(vmem())
        shapes = [jax.ShapeDtypeStruct((heads * T, D), bf16)] * Y
        out_specs = [vmem()] * Y
        if final:
            span = final[1] - final[0]
            for d in range(Z):
                shape = ((span - d + Z - 1) // Z, *block)
                shapes.append(jax.ShapeDtypeStruct(shape, bf16 if d else f32))
                out_specs.append(vmem())
        if left:
            for _ in range(2):
                shape = ((left[1] - left[0]) * T, D)
                shapes.append(jax.ShapeDtypeStruct(shape, f32))
                out_specs.append(vmem())
        held = (hi - lo) * T
        return pl.pallas_call(
            functools.partial(
                backward, heads, first_row, lo, hi, carried, final, left
            ),
            grid=(count,),
            out_shape=shapes,
            in_specs=in_specs,
            out_specs=out_specs,
            scratch_shapes=[
                pltpu.VMEM((held, D), bf16),
                pltpu.VMEM((D, held), bf16),
                pltpu.VMEM((held, D), bf16),
                pltpu.VMEM((held, D), f32),
                pltpu.VMEM((held, D), f32),
                pltpu.VMEM((2, SPAN, 2 * T), f32),
                pltpu.VMEM((heads, SPAN, T), bf16),
                pltpu.VMEM((heads, SPAN, T), bf16),
                pltpu.VMEM((8, T), f32),
                pltpu.VMEM((tall, D), bf16),
                pltpu.VMEM((heads * T, D), bf16),
            ],
            compiler_params=limit(20),
            cost_estimate=pl.CostEstimate(
                flops=10 * count * heads * T * SPAN * D,
                transcendentals=count * heads * T * SPAN,
                bytes_accessed=8 << 20,
            ),
        )(*operands)

    first, second, third = HALO * Z, (HALO + 1) * Z, POS
    *dq_a, dk, dv = run(moved[0], 0, Y, 0, POS, (), (), None, (0, POS), None)
    *rest, dk1, dv1 = run(
        moved[1],
        0,
        2,
        0,
        first + 5,
        ((0, first + 5, 0),),
        (dk, dv),
        (0, first),
        (first, first + 5),
        None,
    )
    dq_b, dx1, dy1 = rest[:Y], rest[Y], rest[Y + 1 :]
    *rest, dk2, dv2 = run(
        moved[1],
        2,
        1,
        first,
        second + 5,
        ((first, first + 5, first), (first + 5, second + 5, 0)),
        (dk1, dv1, dk, dv),
        (first, second),
        (second, second + 5),
        dq_b,
    )
    dq_b, dx2, dy2 = rest[:Y], rest[Y], rest[Y + 1 :]
    rest = run(
        moved[1],
        3,
        1,
        second,
        third,
        ((second, second + 5, second), (second + 5, third, 0)),
        (dk2, dv2, dk, dv),
        (second, third),
        None,
        dq_b,
    )
    dq_b, dx3, dy3 = rest[:Y], rest[Y], rest[Y + 1 :]

    backs = []
    for dys in (dy1, dy2, dy3):
        for d in range(1, Z):
            backs.append(lax.ppermute(dys[d - 1], "z", against(d)))
    halo_out = pl.pallas_call(
        halo_sum,
        out_shape=jax.ShapeDtypeStruct((HALO, *block), bf16),
        in_specs=[vmem()] * 4,
        out_specs=vmem(),
        scratch_shapes=[pltpu.VMEM((HALO + 1, *block), f32)],
        compiler_params=limit(4),
    )(dx1, *backs[: Z - 1])
    halo_back = lax.ppermute(
        halo_out, "blk", [(b + 1, b) for b in range(0, blks - 1, 2)]
    )
    far_back = lax.ppermute(
        halo_out, "blk", [(b + 1, b) for b in range(1, blks - 1, 2)]
    )
    back_a = swap(dq_a, back_from)
    back_b = swap(dq_b, back_from)
    dkv = simple(
        own_sum, [shape(*block)] * Y, 13, 8, [pltpu.VMEM((ROWS, *block), f32)]
    )(dx2, dx3, halo_back, far_back, *backs)
    dkv = swap(dkv, back_from)
    dq_out = simple(
        functools.partial(unpack_q, heads), shape(rows, Y * group * D), PARTS * Y, 8
    )(*back_a, *back_b)
    dk_out, dv_out = simple(unpack_kv, [shape(rows, Y * D)] * 2, Y, 4)(*dkv)
    return dq_out, dk_out, dv_out


def solution(mesh):
    fine = Mesh(mesh.devices.reshape(4, 4, Y, Z), AXES)
    split = P(AXES, None)

    return jax.shard_map(
        on_device,
        mesh=fine,
        in_specs=(split,) * 5 + (P("batch"),),
        out_specs=(split,) * 3,
        check_vma=False,
    )
```

```python
import functools

import jax
import jax.numpy as jnp
from jax import lax
from jax.experimental import pallas as pl
from jax.experimental.pallas import tpu as pltpu
from jax.sharding import Mesh
from jax.sharding import PartitionSpec as P


D = 128
T = 128
WINDOW = 1024
Y = 4
Z = 4
BACK = WINDOW // T
POS = BACK + Z * (Y - 1) + 1
ROWS = BACK // Z + Y
SPAN = (BACK + 1) * T
HALO = BACK // Z
EARLY = 2
PARTS = 2
SCALE = D**-0.5
LOG2E = 1.4426950408889634
AXES = ("batch", "blk", "y", "z")


def ring(e):
    return (lax.axis_index("y") + e) & (Y - 1)


def lanes(block, width):
    return pl.ds(pl.multiple_of(block * width, width), width)


def pack_kv(k_hbm, v_hbm, *refs):
    *outs, k_buf, v_buf, sems = refs
    copies = [
        pltpu.make_async_copy(k_hbm, k_buf, sems.at[0]),
        pltpu.make_async_copy(v_hbm, v_buf, sems.at[1]),
    ]
    for copy in copies:
        copy.start()
    for copy in copies:
        copy.wait()
    for e, out in enumerate(outs):
        cols = lanes(ring(e), D)
        out[:T] = k_buf[:, cols]
        out[T:] = v_buf[:, cols]


def arrange(a_ref, b_ref, c_ref, d_ref, own_ref, tail_ref, *lates):
    for e, ref in enumerate((a_ref, b_ref, c_ref, d_ref)):
        own_ref[pl.ds(ring(-e), 1)] = ref[...][None]
    tail_ref[...] = own_ref[Y - HALO :]
    z = lax.axis_index("z")
    for d, late in enumerate(lates, 1):
        count = late.shape[0]
        off = Y - count - 1 + (z < d).astype(jnp.int32)
        late[...] = own_ref[pl.ds(off, count)]


def arrange_early(own_ref, halo_ref, *earlies):
    z = lax.axis_index("z")
    for d, early in enumerate(earlies, 1):
        near = z < d

        @pl.when(near)
        def _():
            early[: HALO - 1] = halo_ref[1:]
            early[HALO - 1 :] = own_ref[: EARLY - HALO + 1]

        @pl.when(jnp.logical_not(near))
        def _():
            early[...] = halo_ref[...]


def pack_rows(heads, part, q_hbm, s_hbm, g_hbm, *refs):
    *outs, q_buf, s_buf, g_buf, sems = refs
    wide = heads * D
    copies = []
    for e in range(len(outs)):
        cols = lanes(ring(e) * PARTS + part, wide)
        for i, (hbm, buf) in enumerate(
            ((g_hbm, g_buf), (s_hbm, s_buf), (q_hbm, q_buf))
        ):
            copies.append(
                pltpu.make_async_copy(hbm.at[:, cols], buf.at[e], sems.at[e, i])
            )
            copies[-1].start()
    for e, out in enumerate(outs):
        for copy in copies[3 * e : 3 * e + 3]:
            copy.wait()
        deltas = []
        for h in range(heads):
            cols = slice(h * D, (h + 1) * D)
            out[h * T : (h + 1) * T] = q_buf[e, :, cols]
            grad = g_buf[e, :, cols]
            out[(heads + h) * T : (heads + h + 1) * T] = grad
            product = grad.astype(jnp.float32) * s_buf[e, :, cols].astype(jnp.float32)
            deltas.append(jnp.sum(product.T, axis=0, keepdims=True))
        deltas.append(jnp.zeros((8 - heads, T), jnp.float32))
        out[2 * heads * T :] = jnp.concatenate(deltas, axis=0).astype(jnp.bfloat16)


def key_block(p, own, halo, early, late):
    m, d = divmod(p, Z)
    if d == 0:
        return halo[m] if m < HALO else own[m - HALO]
    return early[d - 1][m] if m < EARLY else late[d - 1][m - EARLY]


def backward(heads, first_row, lo, hi, carried, finals, left, builds, joins, key_base, *refs):
    refs = list(refs)
    doc_ref, *row_refs = refs[: 1 + Y]
    refs = refs[1 + Y :]
    halo, early = None, None
    if builds:
        own, late, refs = refs[0], refs[1:4], refs[4:]
        if lo < HALO * Z:
            halo, early, refs = refs[0], refs[1:4], refs[4:]
    else:
        (k_scr, kt_scr, v_scr), refs = refs[:3], refs[3:]
    acc_in = []
    for _ in carried:
        acc_in.append((refs.pop(0), refs.pop(0)))
    dq_before, refs = (refs[:Y], refs[Y:]) if joins else ([], refs)
    dq_refs, refs = refs[:Y], refs[Y:]
    targets = [[refs.pop(0) for _ in range(Z)] for _ in finals]
    acc_out = (refs.pop(0), refs.pop(0)) if left else ()
    if builds:
        dk_scr, dv_scr = acc_out
        (k_scr, kt_scr, v_scr), refs = refs[:3], refs[3:]
    else:
        dk_scr, dv_scr, refs = refs[0], refs[1], refs[2:]
    s_scr, p_scr, ds_scr, delta_scr, row_ref, dq_ref = refs
    step = pl.program_id(0)

    @pl.when(step == 0)
    def _():
        if builds:
            for p in range(lo, hi):
                at = slice((p - lo) * T, (p - lo + 1) * T)
                block = key_block(p, own, halo, early, late)
                key = block[:T]
                k_scr[at] = key
                kt_scr[:, at] = key.astype(jnp.float32).T.astype(jnp.bfloat16)
                v_scr[at] = block[T:]
        for before, dq_out in zip(dq_before, dq_refs):
            dq_out[...] = before[...]
        if sum(end - begin for begin, end, _ in carried) < hi - lo:
            dk_scr[...] = jnp.zeros_like(dk_scr)
            dv_scr[...] = jnp.zeros_like(dv_scr)
        for (begin, end, base), (dk_in, dv_in) in zip(carried, acc_in):
            to = slice((begin - lo) * T, (end - lo) * T)
            at = slice((begin - base) * T, (end - base) * T)
            dk_scr[to] = dk_in[at]
            dv_scr[to] = dv_in[at]

    source = ring(-first_row - step)
    for e in range(Y):

        @pl.when(source == e)
        def _():
            row_ref[...] = row_refs[e][...]

    delta_scr[...] = row_ref[2 * heads * T :, :].astype(jnp.float32)
    slab = Y * Z * T
    base = lax.axis_index("blk") * slab + (lax.axis_index("z") - BACK + lo) * T
    first = pl.multiple_of(step * (Z * T), Z * T)
    query = first + WINDOW + lax.broadcasted_iota(jnp.int32, (1, T), 1)
    start = jnp.zeros((1, T), jnp.int32)
    bound = 0
    for c in range(7):
        bound = bound + doc_ref[c]
        start = jnp.where(query + base >= bound, bound, start)
    lowest = jnp.maximum(start - base, query - (WINDOW - 1)) - first
    lowest = jnp.concatenate([lowest, lowest], axis=1)
    key_at = lax.broadcasted_iota(jnp.int32, (T, 2 * T), 0)
    query_at = lax.broadcasted_iota(jnp.int32, (T, 2 * T), 1) & (T - 1)

    span = pl.ds(first, SPAN)
    seen = pl.ds(pl.multiple_of(first + (lo - key_base) * T, T), SPAN)

    def scores(j):
        at = slice(j * 2 * T, (j + 1) * 2 * T)
        s_all = lax.dot_general(
            k_scr[seen, :],
            row_ref[at, :],
            (((1,), (1,)), ((), ())),
            preferred_element_type=jnp.float32,
        )
        top = jnp.full((8, 2 * T), -1e30, jnp.float32)
        for c in range(BACK + 1):
            rows = slice(c * T, (c + 1) * T)
            allowed = key_at >= lowest - c * T
            if c == BACK:
                allowed = allowed & (key_at <= query_at)
            s = jnp.where(allowed, s_all[rows], -1e30)
            s_scr[j % 2, rows] = s
            for r in range(T // 8):
                top = jnp.maximum(top, s[r * 8 : (r + 1) * 8])
        return jnp.max(top, axis=0, keepdims=True) * (SCALE * LOG2E)

    def exponentials(j, peak):
        total = jnp.zeros((8, 2 * T), jnp.float32)
        for c in range(BACK + 1):
            rows = slice(c * T, (c + 1) * T)
            e = jnp.exp2(s_scr[j % 2, rows] * (SCALE * LOG2E) - peak)
            s_scr[j % 2, rows] = e
            for r in range(T // 8):
                total = total + e[r * 8 : (r + 1) * 8]
        return 1.0 / jnp.sum(total, axis=0, keepdims=True)

    def gradients(j, inverse):
        delta = jnp.concatenate(
            [delta_scr[2 * j : 2 * j + 1], delta_scr[2 * j + 1 : 2 * j + 2]], axis=1
        )
        dp_all = lax.dot_general(
            v_scr[seen, :],
            row_ref[heads * T + j * 2 * T : heads * T + (j + 1) * 2 * T, :],
            (((1,), (1,)), ((), ())),
            preferred_element_type=jnp.float32,
        )
        for c in range(BACK + 1):
            rows = slice(c * T, (c + 1) * T)
            p = s_scr[j % 2, rows] * inverse
            ds = p * (dp_all[rows] - delta)
            for i in range(2):
                cols = slice(i * T, (i + 1) * T)
                p_scr[2 * j + i, rows] = p[:, cols].astype(jnp.bfloat16)
                ds_scr[2 * j + i, rows] = ds[:, cols].astype(jnp.bfloat16)

    def joined(ref, heads_of):
        return jnp.concatenate([ref[h] for h in heads_of], axis=1)

    def products(heads_of):
        n = len(heads_of)
        at = heads_of[0] * T
        dv_scr[span, :] += jnp.dot(
            joined(p_scr, heads_of),
            row_ref[heads * T + at : heads * T + at + n * T, :],
            preferred_element_type=jnp.float32,
        )
        ds = joined(ds_scr, heads_of)
        dk_scr[span, :] += jnp.dot(
            ds, row_ref[at : at + n * T, :], preferred_element_type=jnp.float32
        )
        dqt = jnp.dot(kt_scr[:, seen], ds, preferred_element_type=jnp.float32)
        for i, h in enumerate(heads_of):
            dq_ref[h * T : (h + 1) * T] = (
                (dqt[:, i * T : (i + 1) * T] * SCALE).T.astype(jnp.bfloat16)
            )

    pairs = heads // 2
    inverse = exponentials(0, scores(0))
    for j in range(pairs):
        peak = scores(j + 1) if j + 1 < pairs else None
        gradients(j, inverse)
        if j + 1 < pairs:
            inverse = exponentials(j + 1, peak)
    products(range(heads))

    for e in range(Y):

        @pl.when(source == e)
        def _():
            dq_refs[e][...] = dq_ref[...]

    @pl.when(step == pl.num_programs(0) - 1)
    def _():
        for (begin, end), group in zip(finals, targets):
            for p in range(begin, end):
                m, d = divmod(p - begin, Z)
                at = slice((p - lo) * T, (p - lo + 1) * T)
                target = group[d]
                target[m, :T] = (dk_scr[at] * SCALE).astype(target.dtype)
                target[m, T:] = dv_scr[at].astype(target.dtype)
        if left and not builds:
            at = slice((left[0] - lo) * T, (left[1] - lo) * T)
            acc_out[0][...] = dk_scr[at]
            acc_out[1][...] = dv_scr[at]


def halo_sum(dx_ref, a_ref, b_ref, c_ref, o_ref, acc):
    z = lax.axis_index("z")
    acc[:HALO] = dx_ref[...]
    for d, ref in ((1, a_ref), (2, b_ref), (3, c_ref)):
        off = (z < d).astype(jnp.int32)
        for m in range(HALO):
            acc[off + m] += ref[m].astype(jnp.float32)
    o_ref[...] = acc[:HALO].astype(jnp.bfloat16)


def own_sum(dx_ref, more_ref, halo_ref, far_ref, *refs):
    backs, outs, acc = refs[: 3 * (Z - 1)], refs[3 * (Z - 1) : -1], refs[-1]
    z = lax.axis_index("z")
    acc[:HALO] = jnp.zeros((HALO, 2 * T, D), jnp.float32)
    acc[HALO : HALO + 1] = dx_ref[...]
    acc[HALO + 1 :] = more_ref[...]
    for d in range(1, Z):
        off = (z < d).astype(jnp.int32)
        one, two, three = backs[d - 1 :: Z - 1]
        acc[off + HALO - 1] += one[HALO - 1].astype(jnp.float32)
        acc[off + HALO] += two[0].astype(jnp.float32)
        for m in range(three.shape[0]):
            acc[off + HALO + 1 + m] += three[m].astype(jnp.float32)
    acc[ROWS - HALO :] += (halo_ref[...] + far_ref[...]).astype(jnp.float32)
    for e, out in enumerate(outs):
        out[...] = acc[HALO + ring(-e)].astype(jnp.bfloat16)


def unpack_q(heads, *refs):
    *parts, o_ref = refs
    for i, ref in enumerate(parts):
        part, e = divmod(i, Y)
        for h in range(heads):
            cols = lanes((ring(e) * PARTS + part) * heads + h, D)
            o_ref[:, cols] = ref[h * T : (h + 1) * T]


def unpack_kv(a_ref, b_ref, c_ref, d_ref, k_ref, v_ref):
    for e, ref in enumerate((a_ref, b_ref, c_ref, d_ref)):
        cols = lanes(ring(e), D)
        k_ref[:, cols] = ref[:T]
        v_ref[:, cols] = ref[T:]


def vmem():
    return pl.BlockSpec(memory_space=pltpu.VMEM)


def limit(mib):
    return pltpu.CompilerParams(vmem_limit_bytes=mib << 20)


def on_device(queries, keys, values, saved_out, out_grad, doc_lengths):
    rows = queries.shape[0]
    group = queries.shape[1] // keys.shape[1]
    heads = group // PARTS
    bf16, f32 = jnp.bfloat16, jnp.float32
    blks = lax.axis_size("blk")
    block = (2 * T, D)

    def along(d):
        return [(i, (i - d) % Z) for i in range(Z)]

    def against(d):
        return [((i - d) % Z, i) for i in range(Z)]

    def out_of(e):
        return [(i, (i + e) % Y) for i in range(Y)]

    def back_from(e):
        return [((i + e) % Y, i) for i in range(Y)]

    def shape(*dims, dtype=bf16):
        return jax.ShapeDtypeStruct(dims, dtype)

    def simple(body, shapes, count, mib, scratch=()):
        return pl.pallas_call(
            body,
            out_shape=shapes,
            in_specs=[vmem()] * count,
            out_specs=jax.tree.map(lambda _: vmem(), shapes),
            scratch_shapes=scratch,
            compiler_params=limit(mib),
        )

    def swap(pieces, pairs):
        out = [pieces[0]]
        for e in range(1, Y):
            out.append(lax.ppermute(pieces[e], "y", pairs(e)))
        return out

    count = ROWS - 1 - EARLY
    kv = pl.pallas_call(
        pack_kv,
        out_shape=[shape(*block)] * Y,
        in_specs=[pl.BlockSpec(memory_space=pltpu.HBM)] * 2,
        out_specs=[vmem()] * Y,
        scratch_shapes=[pltpu.VMEM((T, Y * D), bf16)] * 2
        + [pltpu.SemaphoreType.DMA((2,))],
        compiler_params=limit(56),
    )(keys, values)
    kv = swap(kv, out_of)
    own, tail, *lates = simple(
        arrange,
        [shape(Y, *block), shape(HALO, *block)] + [shape(count, *block)] * (Z - 1),
        Y,
        4,
    )(*kv)
    halo = lax.ppermute(tail, "blk", [(b, b + 1) for b in range(blks - 1)])
    late = []
    for d in range(1, Z):
        late.append(lax.ppermute(lates[d - 1], "z", along(d)))
    tall = 2 * heads * T + 8
    moved, packs = [], []
    for part in range(PARTS):
        packed = pl.pallas_call(
            functools.partial(pack_rows, heads, part),
            out_shape=[shape(tall, D)] * Y,
            in_specs=[pl.BlockSpec(memory_space=pltpu.HBM)] * 3,
            out_specs=[vmem()] * Y,
            scratch_shapes=[pltpu.VMEM((Y, T, heads * D), bf16)] * 3
            + [pltpu.SemaphoreType.DMA((Y, 3))],
            compiler_params=limit(56),
        )(queries, saved_out, out_grad)
        packs.append(list(packed))
    halo, packs[1][0] = lax.optimization_barrier((halo, packs[1][0]))
    earlies = simple(arrange_early, [shape(EARLY, *block)] * (Z - 1), 2, 4)(own, halo)
    early = []
    for d in range(1, Z):
        early.append(lax.ppermute(earlies[d - 1], "z", along(d)))

    for packed in packs:
        moved.append(swap(packed, out_of))

    def run(
        row, first_row, count, lo, hi, carried, accs, finals, left, dq, seen, base
    ):
        builds = len(seen) > 3
        operands = [doc_lengths, *row, *seen]
        in_specs = [pl.BlockSpec(memory_space=pltpu.SMEM)]
        in_specs += [vmem() for a in operands[1:]]
        for a in accs:
            operands.append(a)
            in_specs.append(vmem())
        for before in dq:
            operands.append(before)
            in_specs.append(vmem())
        shapes = [jax.ShapeDtypeStruct((heads * T, D), bf16)] * Y
        out_specs = [vmem()] * Y
        for begin, end in finals:
            span = end - begin
            for d in range(Z):
                shape = ((span - d + Z - 1) // Z, *block)
                shapes.append(jax.ShapeDtypeStruct(shape, bf16 if d else f32))
                out_specs.append(vmem())
        if left:
            for _ in range(2):
                shape = ((left[1] - left[0]) * T, D)
                shapes.append(jax.ShapeDtypeStruct(shape, f32))
                out_specs.append(vmem())
        held = (hi - lo) * T
        scratch = [pltpu.VMEM((held, D), f32)] * 2
        if builds:
            scratch = []
            for shape in ((held, D), (D, held), (held, D)):
                shapes.append(jax.ShapeDtypeStruct(shape, bf16))
                out_specs.append(vmem())
        return pl.pallas_call(
            functools.partial(
                backward,
                heads,
                first_row,
                lo,
                hi,
                carried,
                finals,
                left,
                builds,
                bool(dq),
                base,
            ),
            grid=(count,),
            out_shape=shapes,
            in_specs=in_specs,
            out_specs=out_specs,
            scratch_shapes=scratch
            + [
                pltpu.VMEM((2, SPAN, 2 * T), f32),
                pltpu.VMEM((heads, SPAN, T), bf16),
                pltpu.VMEM((heads, SPAN, T), bf16),
                pltpu.VMEM((8, T), f32),
                pltpu.VMEM((tall, D), bf16),
                pltpu.VMEM((heads * T, D), bf16),
            ],
            compiler_params=limit(20),
            cost_estimate=pl.CostEstimate(
                flops=10 * count * heads * T * SPAN * D,
                transcendentals=count * heads * T * SPAN,
                bytes_accessed=8 << 20,
            ),
        )(*operands)

    one, two, three_at = HALO * Z, (HALO + 1) * Z, (HALO + 1) * Z + BACK // 2 + 1
    *dq_a, dkl, dvl, k_far, kt_far, v_far = run(
        moved[0], 2, 2, one, POS, (), (), (), (one, POS), (), (own, *late), one
    )
    *dq_a, dk, dv, k_near, kt_near, v_near = run(
        moved[0],
        0,
        2,
        0,
        three_at,
        ((one, three_at, one),),
        (dkl, dvl),
        (),
        (0, three_at),
        dq_a,
        (own, *late, halo, *early),
        0,
    )
    *rest, dk1, dv1 = run(
        moved[1],
        0,
        3,
        0,
        three_at,
        ((0, three_at, 0),),
        (dk, dv),
        ((0, one), (one, two)),
        (two, three_at),
        (),
        (k_near, kt_near, v_near),
        0,
    )
    dq_b, (dx1, *dy1), (dx2, *dy2) = rest[:Y], rest[Y : Y + Z], rest[Y + Z :]
    rest = run(
        moved[1],
        3,
        1,
        two,
        POS,
        ((two, three_at, two), (three_at, POS, one)),
        (dk1, dv1, dkl, dvl),
        ((two, POS),),
        None,
        dq_b,
        (k_far, kt_far, v_far),
        one,
    )
    dq_b, dx3, dy3 = rest[:Y], rest[Y], rest[Y + 1 :]

    backs = []
    for dys in (dy1, dy2, dy3):
        for d in range(1, Z):
            backs.append(lax.ppermute(dys[d - 1], "z", against(d)))
    halo_out = pl.pallas_call(
        halo_sum,
        out_shape=jax.ShapeDtypeStruct((HALO, *block), bf16),
        in_specs=[vmem()] * 4,
        out_specs=vmem(),
        scratch_shapes=[pltpu.VMEM((HALO + 1, *block), f32)],
        compiler_params=limit(4),
    )(dx1, *backs[: Z - 1])
    halo_back = lax.ppermute(
        halo_out, "blk", [(b + 1, b) for b in range(0, blks - 1, 2)]
    )
    far_back = lax.ppermute(
        halo_out, "blk", [(b + 1, b) for b in range(1, blks - 1, 2)]
    )
    back_a = swap(dq_a, back_from)
    back_b = swap(dq_b, back_from)
    dkv = simple(
        own_sum, [shape(*block)] * Y, 13, 8, [pltpu.VMEM((ROWS, *block), f32)]
    )(dx2, dx3, halo_back, far_back, *backs)
    dkv = swap(dkv, back_from)
    dq_out = simple(
        functools.partial(unpack_q, heads), shape(rows, Y * group * D), PARTS * Y, 8
    )(*back_a, *back_b)
    dk_out, dv_out = simple(unpack_kv, [shape(rows, Y * D)] * 2, Y, 4)(*dkv)
    return dq_out, dk_out, dv_out


def solution(mesh):
    fine = Mesh(mesh.devices.reshape(4, 4, Y, Z), AXES)
    split = P(AXES, None)

    return jax.shard_map(
        on_device,
        mesh=fine,
        in_specs=(split,) * 5 + (P("batch"),),
        out_specs=(split,) * 3,
        check_vma=False,
    )
```
